256 devices in a mesh: dp: 64 (over z_lo, y, x, core), ckpt: 4 (over z_hi).
Axes of the slice: x: 4, y: 4, z: 8 (z_hi: 4, z_lo: 2; z = z_hi * 2 + z_lo), core: 2. Of those that a mesh axis runs over, the one named last changes fastest.
Arguments:
- layer_input: bfloat16 [32768, 6144], P(('dp', 'ckpt')), may hold values from -6 to 6
- out_grad: bfloat16 [32768, 6144], P(('dp', 'ckpt')), may hold values from -6 to 6
- router_weight: bfloat16 [32768], P(('dp', 'ckpt')), may hold values from 0.049804688 to 1
- token_slot: int32 [32768], P(('dp', 'ckpt')), may hold values from -1 to 7, as said below
- slot_token: int32 [2048], P(('dp', 'ckpt')), may hold values from -1 to 127, as said below
- gate_weight: bfloat16 [6144, 8192], P('ckpt', 'dp'), may hold values from -0.078125 to 0.078125
- up_weight: bfloat16 [6144, 8192], P('ckpt', 'dp'), may hold values from -0.078125 to 0.078125
- down_weight: bfloat16 [6144, 8192], P('ckpt', 'dp'), may hold values from -0.078125 to 0.078125
Outputs:
- input_grad: bfloat16 [32768, 6144], P(('dp', 'ckpt'))
- router_grad: float32 [32768], P(('dp', 'ckpt'))
- gate_grad: float32 [6144, 8192], P('ckpt', 'dp')
- up_grad: float32 [6144, 8192], P('ckpt', 'dp')
- down_grad: float32 [6144, 8192], P('ckpt', 'dp')
The draws below stay inside these ranges and needn't reach their ends.
Inputs may be any that keep to these rules, and one draw needn't show every extreme that they name: `token_slot`: for each token, its row among the rows that its device sends to the expert, or -1 if the router did not send it there. A device's live rows are 0 to n - 1 for some n of 1 to 8. For each of a device's 8 rows, the index among that device's tokens of the token in it, or -1 for an empty row. Live rows come first; token_slot and slot_token are inverse to each other. In every draw all devices of some group along ckpt fill all 8 rows.
All inputs are finite; a program needn't handle non-finite values.
Results may differ from the reference program's by a relative error of at most 0.0049.
Values may be sent and summed in bfloat16 or wider, within the bound.
A program may use at most 128 MiB of HBM per device.

```python
import math
import jax
import jax.numpy as jnp

D = 6144
CAP = 8
TOK_DEV = 128
HIDDEN_UNITS = 8192
TOKENS = 32768
ROWS = 2048
N_DP = 64
N_CKPT = 4


def routing_tables(key):
    base_key = jax.random.fold_in(key, 7)
    key_count, key_group, key_single, key_scores = jax.random.split(base_key, 4)
    devices = TOKENS // TOK_DEV
    counts = jax.random.randint(key_count, (devices,), (CAP + 1) // 2, CAP + 1)
    full_group = jax.random.randint(key_group, (), 0, devices // N_CKPT)
    single_device = jax.random.randint(key_single, (), 0, devices)
    device_ids = jnp.arange(devices, dtype=jnp.int32)
    filled = (device_ids // N_CKPT == full_group) | (device_ids == single_device)
    counts = jnp.where(filled, CAP, counts)
    scores = jax.random.randint(key_scores, (devices, TOK_DEV), 0, 1 << 16) * TOK_DEV + jnp.arange(TOK_DEV, dtype=jnp.int32)[None, :]
    ranking = jnp.argsort(scores, axis=1, stable=True).astype(jnp.int32)
    position = jnp.argsort(ranking, axis=1, stable=True).astype(jnp.int32)
    slot_table = jnp.where(jnp.arange(CAP, dtype=jnp.int32)[None, :] < counts[:, None], ranking[:, :CAP], -1)
    token_table = jnp.where(position < counts[:, None], position, -1)
    return (token_table.reshape(-1).astype(jnp.int32), slot_table.reshape(-1).astype(jnp.int32))


def draw_token_slot(key, part):
    return routing_tables(key)[0]


def draw_slot_token(key, part):
    return routing_tables(key)[1]


def block_levels(own_key, extent, shards, least, largest):
    factor_of = 1.0
    for axis_at, shards_of in shards:
        steps = jax.random.uniform(jax.random.fold_in(jax.random.fold_in(own_key, 6), axis_at), (shards_of,), jnp.float32, least / len(shards), largest / len(shards))
        factor_of = factor_of * jnp.repeat(jnp.exp(steps), extent[axis_at] // shards_of).reshape((-1,) + (1,) * (len(extent) - 1 - axis_at))
    return factor_of


def centred(rng, shape, width, limit, cuts=(), held_as=jnp.bfloat16):
    entries = width * jax.random.normal(rng, shape, jnp.float32)
    if cuts:
        entries = entries * block_levels(rng, shape, cuts, -0.22, 0.18)
    return jnp.clip(entries, -limit, limit).astype(held_as)


def setup_inputs(seed: int = 0) -> dict:
    seeds = jax.random.split(jax.random.key(seed), 9)
    return {
        "layer_input": centred(seeds[0], (TOKENS, D), 1.0, 6.0, ((0, 256),)),
        "out_grad": centred(seeds[1], (TOKENS, D), 1.0, 6.0, ((0, 256),)),
        "router_weight": jnp.clip(jnp.exp(math.log(1.0) - 2.9996462 * jax.random.uniform(seeds[2], (TOKENS,), jnp.float32) ** block_levels(seeds[2], (TOKENS,), ((0, 256),), -0.2, 0.2)), 0.049804688, 1.0).astype(jnp.bfloat16),
        "token_slot": draw_token_slot(jax.random.fold_in(seeds[8], 71), 0),
        "slot_token": draw_slot_token(jax.random.fold_in(seeds[8], 71), 0),
        "gate_weight": centred(seeds[5], (D, HIDDEN_UNITS), D ** -0.5, 0.078125, ((0, 4), (1, 64))),
        "up_weight": centred(seeds[6], (D, HIDDEN_UNITS), D ** -0.5, 0.078125, ((0, 4), (1, 64))),
        "down_weight": centred(seeds[7], (D, HIDDEN_UNITS), D ** -0.5, 0.078125, ((0, 4), (1, 64))),
    }


def reference(layer_input, out_grad, router_weight, token_slot, slot_token, gate_weight, up_weight, down_weight):
    devices = N_DP * N_CKPT
    inputs = layer_input.reshape(devices, TOK_DEV, D)
    grads = out_grad.reshape(devices, TOK_DEV, D)
    routers = router_weight.reshape(devices, TOK_DEV)
    tokens_map = token_slot.reshape(devices, TOK_DEV)
    slots_map = slot_token.reshape(devices, CAP)
    is_live = slots_map >= 0
    safe_index = jnp.maximum(slots_map, 0).astype(jnp.int32)
    rows_in = jnp.take_along_axis(inputs, safe_index[:, :, None], axis=1)
    rows_in = jnp.where(is_live[:, :, None], rows_in, jnp.zeros((), jnp.bfloat16)).reshape(ROWS, D)
    rows_out = jnp.take_along_axis(grads, safe_index[:, :, None], axis=1)
    rows_out = jnp.where(is_live[:, :, None], rows_out, jnp.zeros((), jnp.bfloat16)).reshape(ROWS, D)
    rows_router = jnp.where(is_live, jnp.take_along_axis(routers, safe_index, axis=1), jnp.zeros((), jnp.bfloat16)).reshape(ROWS)
    gate_pre = jnp.dot(rows_in, gate_weight, preferred_element_type=jnp.float32)
    up_pre = jnp.dot(rows_in, up_weight, preferred_element_type=jnp.float32)
    act_grad = jnp.dot(rows_out, down_weight, preferred_element_type=jnp.float32)
    sigmoid_g = jax.nn.sigmoid(gate_pre)
    active = sigmoid_g * gate_pre * up_pre
    router_f = rows_router.astype(jnp.float32)[:, None]
    scaled = (router_f * active).astype(jnp.bfloat16)
    router_rows = jnp.sum(active * act_grad, axis=1)
    act_delta = router_f * act_grad
    gate_delta = (act_delta * up_pre * sigmoid_g * (1.0 + gate_pre * (1.0 - sigmoid_g))).astype(jnp.bfloat16)
    up_delta = (act_delta * sigmoid_g * gate_pre).astype(jnp.bfloat16)
    input_rows = jnp.dot(gate_delta, gate_weight.T, preferred_element_type=jnp.float32)
    input_rows = (input_rows + jnp.dot(up_delta, up_weight.T, preferred_element_type=jnp.float32)).astype(jnp.bfloat16)
    has_row = tokens_map >= 0
    row_index = (jnp.maximum(tokens_map, 0) + (jnp.arange(devices, dtype=jnp.int32) * CAP)[:, None]).astype(jnp.int32)
    input_tok = jnp.where(has_row[:, :, None], input_rows[row_index], jnp.zeros((), jnp.bfloat16))
    router_tok = jnp.where(has_row, router_rows[row_index], jnp.zeros((), jnp.float32))
    gate_grad = jnp.dot(rows_in.T, gate_delta, preferred_element_type=jnp.float32)
    up_grad = jnp.dot(rows_in.T, up_delta, preferred_element_type=jnp.float32)
    down_grad = jnp.dot(rows_out.T, scaled, preferred_element_type=jnp.float32)
    return input_tok.reshape(TOKENS, D), router_tok.reshape(TOKENS), gate_grad, up_grad, down_grad
```

```python
import functools

import jax
import jax.numpy as jnp
from jax import lax
from jax.experimental import pallas as pl
from jax.experimental.pallas import tpu as pltpu
from jax.sharding import PartitionSpec as P

MESH = pl.DeviceIdType.MESH
BF = jnp.bfloat16
F32 = jnp.float32

RIGHT, LEFT, OPP = 1, 2, 3
OFFSET = (0, 1, 3, 2)
MIRROR = (0, 2, 1, 3)
QUARTER = 1536
EXTRA = 128
WIDE = QUARTER + EXTRA
HID = 128
SLOTS = 8
SHARD = 32
UNITS = 160


def kernel(
    slot_ref,
    router_ref,
    x_hbm,
    g_hbm,
    wg_hbm,
    wu_hbm,
    wd_hbm,
    rows_out,
    router_out,
    own_gate,
    own_up,
    own_down,
    peer_part,
    xbuf,
    gbuf,
    wcat,
    stage_x,
    stage_g,
    land_x,
    land_g,
    xa,
    ga,
    pre_own,
    pre_right,
    pre_left,
    zs,
    zr,
    dl,
    router_part,
    dmat,
    e_own,
    e_right,
    e_left,
    es,
    er,
    f_own,
    f_right,
    f_left,
    fs,
    fr,
    zl_send,
    zl_recv,
    last_send,
    last_recv,
    part_send,
    send_sem,
    recv_sem,
    local_sem,
):
    g = lax.axis_index("dp")
    m = lax.axis_index("ckpt")
    core = lax.rem(g, 2)
    x = lax.rem(g // 2, 4)
    y = lax.rem(g // 8, 4)
    zlo = g // 32

    def device(dx, dy, dz):
        return (zlo_of(dz) * 32 + lax.rem(y + dy, 4) * 8 + lax.rem(x + dx, 4) * 2 + core, m)

    def zlo_of(dz):
        return 1 - zlo if dz else zlo

    a_right = device(core, 1 - core, 0)
    a_left = device(3 * core, 3 * (1 - core), 0)
    b_right = device(1 - core, core, 0)
    b_left = device(3 * (1 - core), 3 * core, 0)
    partner = device(0, 0, 1)
    sibling = (g + 1 - 2 * core, m)
    z_at = [(g, lax.rem(m + OFFSET[p], 4)) for p in range(4)]
    z_right, z_left = z_at[RIGHT], z_at[LEFT]

    sent = []

    def send(src, dst, to):
        unit = len(sent)
        copy = pltpu.make_async_remote_copy(
            src_ref=src,
            dst_ref=dst,
            send_sem=send_sem.at[unit],
            recv_sem=recv_sem.at[unit],
            device_id=to,
            device_id_type=MESH,
        )
        copy.start()
        sent.append(copy)
        return copy

    locals_ = []

    def local(src, dst):
        copy = pltpu.make_async_copy(src, dst, local_sem.at[len(locals_)])
        copy.start()
        locals_.append(copy)
        return copy

    class Gather:
        def __init__(self, at, right, left):
            self.at, self.right, self.left = at, right, left

        def start(self, half):
            at = self.at
            if half == 0:
                self.r0 = send(at(0, 0), at(LEFT, 0), self.right)
                self.l0 = send(at(0, 0), at(RIGHT, 0), self.left)
            else:
                self.l1 = send(at(0, 1), at(RIGHT, 1), self.left)
                self.r1 = send(at(0, 1), at(LEFT, 1), self.right)

        def relay(self):
            at = self.at
            self.r0.wait_recv()
            self.o0 = send(at(LEFT, 0), at(OPP, 0), self.right)
            self.l1.wait_recv()
            self.o1 = send(at(RIGHT, 1), at(OPP, 1), self.left)

        def finish_right(self):
            self.l0.wait_recv()

        def finish_left(self):
            self.r1.wait_recv()

        def finish_opposite(self):
            self.o0.wait_recv()
            self.o1.wait_recv()

        def finish(self):
            self.finish_right()
            self.finish_left()
            self.finish_opposite()

    class Reduce:
        def __init__(self, src, dst, right, left):
            self.src, self.dst, self.right, self.left = src, dst, right, left
            self.units = [None] * 6

        def one(self, unit):
            to = self.right if unit in (0, 2, 4) else self.left
            self.units[unit] = send(self.src(unit), self.dst(unit), to)

        def start(self):
            for unit in (0, 1, 2, 3):
                self.one(unit)

        def relay(self, add):
            self.units[0].wait_recv()
            add(0)
            self.one(4)
            self.units[1].wait_recv()
            add(1)
            self.one(5)

        def finish(self):
            for unit in (2, 3, 4, 5):
                self.units[unit].wait_recv()

    load_x = local(x_hbm, xbuf)
    load_g = local(g_hbm, gbuf)
    weights = (wg_hbm, wu_hbm, wd_hbm)
    load_w = [local(w, wcat.at[j, :, pl.ds(0, HID)]) for j, w in enumerate(weights)]

    barrier = pltpu.get_barrier_semaphore()
    peers = [a_right, a_left, b_right, b_left, partner, sibling] + z_at[1:]
    for peer in peers:
        pl.semaphore_signal(barrier, inc=1, device_id=peer, device_id_type=MESH)

    row = lax.broadcasted_iota(jnp.int32, (16, 128), 0)
    col = lax.broadcasted_iota(jnp.int32, (16, 128), 1)
    pick = jnp.zeros((16, 128), F32)
    for s in range(SLOTS):
        pick = jnp.where((row == s) & (col == slot_ref[s]), 1.0, pick)
    router_rows = jnp.sum(pick[:SLOTS] * router_ref[...].astype(F32), axis=1, keepdims=True)
    router_tile = jnp.broadcast_to(router_rows, (SLOTS, EXTRA)).astype(BF)
    pick = pick.astype(BF)
    quarters = [pl.ds(pl.multiple_of(lax.rem(m + OFFSET[p], 4) * QUARTER, 128), QUARTER) for p in range(4)]

    def rows_of(buf, p):
        got = jnp.dot(pick, buf[:, quarters[p]], preferred_element_type=F32)
        return got[:SLOTS]

    load_x.wait()
    own_x = rows_of(xbuf, 0)
    for p in (1, 2, 3):
        stage_x[p, :, 0:QUARTER] = rows_of(xbuf, p).astype(BF)
        stage_x[p, :, QUARTER:WIDE] = router_tile
    load_g.wait()
    own_g = rows_of(gbuf, 0)
    for p in (1, 2, 3):
        stage_g[p] = rows_of(gbuf, p).astype(BF)
    stage_x[0, :, 0:QUARTER] = own_x.astype(BF)
    stage_x[0, :, QUARTER:WIDE] = router_tile
    stage_g[0] = own_g.astype(BF)

    pl.semaphore_wait(barrier, len(peers))

    first_x = [send(stage_x.at[p], land_x.at[MIRROR[p]], z_at[p]) for p in (3, 1, 2)]
    first_g = [send(stage_g.at[p], land_g.at[MIRROR[p]], z_at[p]) for p in (3, 1, 2)]
    sent_w = [send(w, wcat.at[j, :, pl.ds(HID, HID)], sibling) for j, w in enumerate(weights)]

    def make_shard(stage, land, out):
        parts = [stage[0].astype(F32)] + [land[p].astype(F32) for p in (1, 2, 3)]
        out[0:16] = jnp.concatenate(parts[0:2], axis=0).astype(BF)
        out[16:32] = jnp.concatenate(parts[2:4], axis=0).astype(BF)

    arrays = (xa, ga)
    gather_b = [Gather(lambda p, h, t=t: t.at[p, 0, h], b_right, b_left) for t in arrays]
    gather_a = [
        [Gather(lambda p, h, t=t, k=k: t.at[k, p, h], a_right, a_left) for t in arrays] for k in range(4)
    ]

    pair = []
    for i, (stage, land, first) in enumerate(((stage_x, land_x, first_x), (stage_g, land_g, first_g))):
        for copy in first:
            copy.wait_recv()
        make_shard(stage, land, arrays[i].at[0, 0, 0])
        pair.append(send(arrays[i].at[0, 0, 0], arrays[i].at[0, 0, 1], partner))
        gather_a[0][i].start(0)
        gather_b[i].start(0)
    for i in range(2):
        pair[i].wait_recv()
        gather_a[0][i].start(1)
        gather_b[i].start(1)

    reduce_z = [Reduce(lambda u, k=k: zs.at[k, u], lambda u, k=k: zr.at[k, u], z_right, z_left) for k in range(4)]
    gather_z = [Gather(lambda p, h, k=k: dl.at[k, p, h], z_right, z_left) for k in range(4)]
    reduce_a = [Reduce(lambda u, k=k: es.at[k, u], lambda u, k=k: er.at[k, u], a_right, a_left) for k in range(4)]
    reduce_b = Reduce(lambda u: fs.at[u], lambda u: fr.at[u], b_right, b_left)

    def forward(k):
        lhs_x = xa[k, :, :, :, 0:QUARTER].reshape(256, QUARTER)
        lhs_g = ga[k].reshape(256, QUARTER)
        for j, lhs in enumerate((lhs_x, lhs_x, lhs_g)):
            pre = jnp.dot(lhs, wcat[j], preferred_element_type=F32)
            piece = [
                [
                    jnp.concatenate([pre[(q * 4 + p) * 8 : (q * 4 + p) * 8 + 8] for q in range(4 * h, 4 * h + 4)], axis=0)
                    for h in range(2)
                ]
                for p in range(4)
            ]
            zs[k, 0, j] = piece[OPP][0]
            zs[k, 1, j] = piece[OPP][1]
            zs[k, 2, j] = piece[RIGHT][1]
            zs[k, 3, j] = piece[LEFT][0]
            pre_own[k, 0, j] = piece[0][0]
            pre_own[k, 1, j] = piece[0][1]
            pre_right[k, j] = piece[RIGHT][0]
            pre_left[k, j] = piece[LEFT][1]
        reduce_z[k].start()

    def relay_z(k):
        def add(side):
            mine = pre_left if side else pre_right
            zs[k, 4 + side] = mine[k] + zr[k, side]

        reduce_z[k].relay(add)

    def elementwise(k):
        reduce_z[k].finish()
        for h in range(2):
            near, far = (2, 5) if h else (3, 4)
            total = pre_own[k, h] + zr[k, near] + zr[k, far]
            gate_pre, up_pre, act_grad = total[0], total[1], total[2]
            router = xa[k, 2 * h : 2 * h + 2, :, 0:16, QUARTER:WIDE].astype(F32)[:, :, 0:8].reshape(32, EXTRA)
            router = jnp.concatenate([router, router], axis=1)
            sigmoid_g = jax.nn.sigmoid(gate_pre)
            active = sigmoid_g * gate_pre * up_pre
            dl[k, 0, h, 2] = (router * active).astype(BF)
            act_delta = router * act_grad
            dl[k, 0, h, 0] = (act_delta * up_pre * sigmoid_g * (1.0 + gate_pre * (1.0 - sigmoid_g))).astype(BF)
            dl[k, 0, h, 1] = (act_delta * sigmoid_g * gate_pre).astype(BF)
            product = active * act_grad
            router_part[k, pl.ds(32 * h, 32)] = product[:, 0:128] + product[:, 128:256]
            gather_z[k].start(h)

    def extra_of(v):
        high = v.astype(BF)
        low = (v - high.astype(F32)).astype(BF)
        return jnp.concatenate([high.astype(F32), low.astype(F32), jnp.zeros((16, EXTRA), F32)], axis=0)

    def backward(k):
        for j in range(3):
            d = dl[k, :, :, j].astype(F32)
            parts = []
            for q in range(8):
                for p in range(4):
                    parts.append(d[p, q // 4, (q % 4) * 8 : (q % 4) * 8 + 8])
            dmat[j, pl.ds(256 * k, 256)] = jnp.concatenate(parts, axis=0).astype(BF)

        def block(n, carry):
            cols = pl.ds(pl.multiple_of(n * 256, 256), 256)
            nt = (((1,), (1,)), ((), ()))
            rows = pl.ds(256 * k, 256)
            dx = lax.dot_general(dmat[0, rows], wcat[0, cols, :], nt, preferred_element_type=F32)
            dx = dx + lax.dot_general(dmat[1, rows], wcat[1, cols, :], nt, preferred_element_type=F32)
            unit = [dx[32 * q : 32 * q + 32] for q in range(8)]
            e_own[k, 0, :, cols] = unit[0]
            e_own[k, 1, :, cols] = unit[1]
            e_right[k, :, cols] = unit[2]
            es[k, 2, :, cols] = unit[3].astype(BF)
            es[k, 3, :, cols] = unit[4].astype(BF)
            e_left[k, :, cols] = unit[5]
            es[k, 0, :, cols] = unit[6].astype(BF)
            es[k, 1, :, cols] = unit[7].astype(BF)
            return carry

        lax.fori_loop(0, QUARTER // 256, block, 0)
        tail = slice(QUARTER, WIDE)
        ex = [extra_of(router_part[k, pl.ds(8 * q, 8)]) for q in range(8)]
        e_own[k, 0, :, tail] = ex[0]
        e_own[k, 1, :, tail] = ex[1]
        e_right[k, :, tail] = ex[2]
        es[k, 2, :, tail] = ex[3].astype(BF)
        es[k, 3, :, tail] = ex[4].astype(BF)
        e_left[k, :, tail] = ex[5]
        es[k, 0, :, tail] = ex[6].astype(BF)
        es[k, 1, :, tail] = ex[7].astype(BF)
        reduce_a[k].start()

    def put(ref, total):
        ref[:, 0:QUARTER] = total[:, 0:QUARTER].astype(BF)
        v = total[0:8, QUARTER:WIDE] + total[8:16, QUARTER:WIDE]
        ref[:, QUARTER:WIDE] = extra_of(v).astype(BF)

    def relay_a(k):
        def add(side):
            mine = e_left if side else e_right
            put(es.at[k, 4 + side], mine[k] + er[k, side].astype(F32))

        reduce_a[k].relay(add)

    def finish_a(k):
        reduce_a[k].finish()
        total = [
            e_own[k, h] + er[k, (3, 2)[h]].astype(F32) + er[k, (4, 5)[h]].astype(F32) for h in range(2)
        ]
        if k == 0:
            f_own[0] = total[0]
            f_own[1] = total[1]
        elif k == RIGHT:
            f_right[...] = total[0]
            put(fs.at[2], total[1])
            reduce_b.one(2)
        elif k == LEFT:
            put(fs.at[3], total[0])
            f_left[...] = total[1]
            reduce_b.one(3)
        else:
            put(fs.at[0], total[0])
            reduce_b.one(0)
            put(fs.at[1], total[1])
            reduce_b.one(1)

    def start_a(k):
        for i in range(2):
            if k == RIGHT:
                gather_b[i].finish_right()
            elif k == LEFT:
                gather_b[i].finish_left()
            else:
                gather_b[i].finish_opposite()
            gather_a[k][i].start(0)
            gather_a[k][i].start(1)

    def relay_gather(k):
        for i in range(2):
            gather_a[k][i].relay()

    def finish_gather(k):
        for i in range(2):
            gather_a[k][i].finish()

    part = []

    def weight_block(n, carry):
        cols = pl.ds(pl.multiple_of(n * 256, 256), 256)
        tn = (((0,), (0,)), ((), ()))
        lhs_x = xa[:, :, :, :, cols].reshape(1024, 256)
        lhs_g = ga[:, :, :, :, cols].reshape(1024, 256)
        for j, (lhs, own) in enumerate(((lhs_x, own_gate), (lhs_x, own_up), (lhs_g, own_down))):
            dw = lax.dot_general(lhs, dmat[j], tn, preferred_element_type=F32)
            own[cols, :] = dw[:, 0:HID]
            part_send[j, cols, :] = dw[:, HID:]
        return carry

    def weight_grads():
        lax.fori_loop(0, QUARTER // 256, weight_block, 0)
        for j in range(3):
            part.append(send(part_send.at[j], peer_part.at[j], sibling))

    for i in range(2):
        gather_a[0][i].relay()
        gather_b[i].relay()
    start_a(RIGHT)
    finish_gather(0)
    for copy in load_w:
        copy.wait()
    for copy in sent_w:
        copy.wait_recv()
    forward(0)
    relay_gather(1)
    start_a(LEFT)
    relay_z(0)
    finish_gather(1)
    forward(1)
    elementwise(0)
    relay_gather(2)
    start_a(OPP)
    relay_z(1)
    gather_z[0].relay()
    elementwise(1)
    finish_gather(2)
    forward(2)
    gather_z[0].finish()
    backward(0)
    relay_gather(3)
    relay_z(2)
    gather_z[1].relay()
    relay_a(0)
    elementwise(2)
    finish_gather(3)
    forward(3)
    gather_z[1].finish()
    backward(1)
    relay_z(3)
    gather_z[2].relay()
    relay_a(1)
    finish_a(0)
    elementwise(3)
    gather_z[2].finish()
    backward(2)
    gather_z[3].relay()
    relay_a(2)
    finish_a(1)
    gather_z[3].finish()
    backward(3)
    finish_a(2)
    relay_a(3)
    weight_grads()
    finish_a(3)

    def add_b(side):
        mine = f_left if side else f_right
        put(fs.at[4 + side], mine[...] + fr[side].astype(F32))

    reduce_b.relay(add_b)
    reduce_b.finish()
    for h in (1, 0):
        total = f_own[h] + fr[(3, 2)[h]].astype(F32) + fr[(4, 5)[h]].astype(F32)
        if h:
            put(zl_send, total)
            swap = send(zl_send, zl_recv, partner)
        else:
            f_own[0] = total
    swap.wait_recv()
    total = f_own[0] + zl_recv[...].astype(F32)
    router_sum = total[0:8, QUARTER:WIDE] + total[8:16, QUARTER:WIDE]
    router_out[...] = jnp.broadcast_to(jnp.sum(router_sum, axis=1, keepdims=True), (SLOTS, EXTRA))
    for p in range(4):
        last_send[p] = total[8 * p : 8 * p + 8, 0:QUARTER].astype(BF)
    last = [send(last_send.at[p], last_recv.at[MIRROR[p]], z_at[p]) for p in (3, 1, 2)]
    rows_out[m] = last_send[0]
    for p, copy in zip((3, 1, 2), last):
        copy.wait_recv()
    for p in (1, 2, 3):
        rows_out[lax.rem(m + OFFSET[p], 4)] = last_recv[p]
    for copy in part:
        copy.wait_recv()
    for copy in sent:
        copy.wait_send()


def local_step(
    layer_input,
    out_grad,
    router_weight,
    token_slot,
    slot_token,
    gate_weight,
    up_weight,
    down_weight,
):
    any_ = pl.BlockSpec(memory_space=pl.ANY)
    vmem = pl.BlockSpec(memory_space=pltpu.VMEM)
    grad = jax.ShapeDtypeStruct((QUARTER, HID), F32)
    rows, router, own_gate, own_up, own_down, peer = pl.pallas_call(
        kernel,
        out_shape=(
            jax.ShapeDtypeStruct((4, SLOTS, QUARTER), BF),
            jax.ShapeDtypeStruct((SLOTS, EXTRA), F32),
            grad,
            grad,
            grad,
            jax.ShapeDtypeStruct((3, QUARTER, HID), F32),
        ),
        in_specs=[pl.BlockSpec(memory_space=pltpu.SMEM), vmem, any_, any_, any_, any_, any_],
        out_specs=(vmem, vmem, vmem, vmem, vmem, any_),
        scratch_shapes=[
            pltpu.VMEM((128, 4 * QUARTER), BF),
            pltpu.VMEM((128, 4 * QUARTER), BF),
            pltpu.VMEM((3, QUARTER, 2 * HID), BF),
            pltpu.VMEM((4, SLOTS, WIDE), BF),
            pltpu.VMEM((4, SLOTS, QUARTER), BF),
            pltpu.VMEM((4, SLOTS, WIDE), BF),
            pltpu.VMEM((4, SLOTS, QUARTER), BF),
            pltpu.VMEM((4, 4, 2, SHARD, WIDE), BF),
            pltpu.VMEM((4, 4, 2, SHARD, QUARTER), BF),
            pltpu.VMEM((4, 2, 3, 32, 256), F32),
            pltpu.VMEM((4, 3, 32, 256), F32),
            pltpu.VMEM((4, 3, 32, 256), F32),
            pltpu.VMEM((4, 6, 3, 32, 256), F32),
            pltpu.VMEM((4, 6, 3, 32, 256), F32),
            pltpu.VMEM((4, 4, 2, 3, 32, 256), BF),
            pltpu.VMEM((4, 64, EXTRA), F32),
            pltpu.VMEM((3, 1024, 256), BF),
            pltpu.VMEM((4, 2, SHARD, WIDE), F32),
            pltpu.VMEM((4, SHARD, WIDE), F32),
            pltpu.VMEM((4, SHARD, WIDE), F32),
            pltpu.VMEM((4, 6, SHARD, WIDE), BF),
            pltpu.VMEM((4, 6, SHARD, WIDE), BF),
            pltpu.VMEM((2, SHARD, WIDE), F32),
            pltpu.VMEM((SHARD, WIDE), F32),
            pltpu.VMEM((SHARD, WIDE), F32),
            pltpu.VMEM((6, SHARD, WIDE), BF),
            pltpu.VMEM((6, SHARD, WIDE), BF),
            pltpu.VMEM((SHARD, WIDE), BF),
            pltpu.VMEM((SHARD, WIDE), BF),
            pltpu.VMEM((4, SLOTS, QUARTER), BF),
            pltpu.VMEM((4, SLOTS, QUARTER), BF),
            pltpu.VMEM((3, QUARTER, HID), F32),
            pltpu.SemaphoreType.DMA((UNITS,)),
            pltpu.SemaphoreType.DMA((UNITS,)),
            pltpu.SemaphoreType.DMA((8,)),
        ],
        compiler_params=pltpu.CompilerParams(
            collective_id=0, has_side_effects=True, vmem_limit_bytes=60 * 1024 * 1024
        ),
    )(slot_token, router_weight[None, :], layer_input, out_grad, gate_weight, up_weight, down_weight)

    slots = jnp.arange(SLOTS, dtype=jnp.int32)
    hit = token_slot[:, None] == slots[None, :]
    flat = rows.transpose(1, 0, 2).reshape(SLOTS, 4 * QUARTER)
    input_grad = jnp.dot(hit.astype(BF), flat, preferred_element_type=F32).astype(BF)
    router_grad = jnp.sum(jnp.where(hit, router[None, :, 0], 0.0), axis=1)
    return (input_grad, router_grad, own_gate + peer[0], own_up + peer[1], own_down + peer[2])


def solution(mesh):
    both = ("dp", "ckpt")
    return jax.shard_map(
        local_step,
        mesh=mesh,
        in_specs=(
            P(both, None),
            P(both, None),
            P(both),
            P(both),
            P(both),
            P("ckpt", "dp"),
            P("ckpt", "dp"),
            P("ckpt", "dp"),
        ),
        out_specs=(P(both, None), P(both), P("ckpt", "dp"), P("ckpt", "dp"), P("ckpt", "dp")),
        check_vma=False,
    )
```

```python
import functools

import jax
import jax.numpy as jnp
from jax import lax
from jax.experimental import pallas as pl
from jax.experimental.pallas import tpu as pltpu
from jax.sharding import PartitionSpec as P

MESH = pl.DeviceIdType.MESH
BF = jnp.bfloat16
F32 = jnp.float32
I32 = jnp.int32
I16 = jnp.int16

RIGHT, LEFT, OPP = 1, 2, 3
OFFSET = (0, 1, 3, 2)
MIRROR = (0, 2, 1, 3)
QUARTER = 1536
EXTRA = 128
WIDE = QUARTER + EXTRA
HID = 128
SLOTS = 8
SHARD = 32
UNITS = 160
CODED = 112
STEPS = 32000.0


def kernel(
    slot_ref,
    router_ref,
    token_ref,
    x_hbm,
    g_hbm,
    wg_hbm,
    wu_hbm,
    wd_hbm,
    input_out,
    router_out,
    gate_out,
    up_out,
    down_out,
    xbuf,
    gbuf,
    wcat,
    stage_x,
    stage_g,
    land_x,
    land_g,
    xa,
    ga,
    pre_own,
    pre_right,
    pre_left,
    zs,
    zr,
    dl,
    router_part,
    dmat,
    e_own,
    e_right,
    e_left,
    es,
    er,
    f_own,
    f_right,
    f_left,
    fs,
    fr,
    zl_send,
    zl_recv,
    last_send,
    last_recv,
    part_send,
    own_part,
    peer_part,
    send_sem,
    recv_sem,
    local_sem,
):
    g = lax.axis_index("dp")
    m = lax.axis_index("ckpt")
    core = lax.rem(g, 2)
    x = lax.rem(g // 2, 4)
    y = lax.rem(g // 8, 4)
    zlo = g // 32

    def device(dx, dy, dz):
        return (zlo_of(dz) * 32 + lax.rem(y + dy, 4) * 8 + lax.rem(x + dx, 4) * 2 + core, m)

    def zlo_of(dz):
        return 1 - zlo if dz else zlo

    a_right = device(core, 1 - core, 0)
    a_left = device(3 * core, 3 * (1 - core), 0)
    b_right = device(1 - core, core, 0)
    b_left = device(3 * (1 - core), 3 * core, 0)
    partner = device(0, 0, 1)
    sibling = (g + 1 - 2 * core, m)
    z_at = [(g, lax.rem(m + OFFSET[p], 4)) for p in range(4)]
    z_right, z_left = z_at[RIGHT], z_at[LEFT]

    sent = []

    def send(src, dst, to):
        unit = len(sent)
        copy = pltpu.make_async_remote_copy(
            src_ref=src,
            dst_ref=dst,
            send_sem=send_sem.at[unit],
            recv_sem=recv_sem.at[unit],
            device_id=to,
            device_id_type=MESH,
        )
        copy.start()
        sent.append(copy)
        return copy

    locals_ = []

    def local(src, dst):
        copy = pltpu.make_async_copy(src, dst, local_sem.at[len(locals_)])
        copy.start()
        locals_.append(copy)
        return copy

    class Gather:
        def __init__(self, at, right, left):
            self.at, self.right, self.left = at, right, left

        def start(self, half):
            at = self.at
            if half == 0:
                self.r0 = send(at(0, 0), at(LEFT, 0), self.right)
                self.l0 = send(at(0, 0), at(RIGHT, 0), self.left)
            else:
                self.l1 = send(at(0, 1), at(RIGHT, 1), self.left)
                self.r1 = send(at(0, 1), at(LEFT, 1), self.right)

        def relay(self):
            at = self.at
            self.r0.wait_recv()
            self.o0 = send(at(LEFT, 0), at(OPP, 0), self.right)
            self.l1.wait_recv()
            self.o1 = send(at(RIGHT, 1), at(OPP, 1), self.left)

        def finish_right(self):
            self.l0.wait_recv()

        def finish_left(self):
            self.r1.wait_recv()

        def finish_opposite(self):
            self.o0.wait_recv()
            self.o1.wait_recv()

        def finish(self):
            self.finish_right()
            self.finish_left()
            self.finish_opposite()

    class Reduce:
        def __init__(self, src, dst, right, left):
            self.src, self.dst, self.right, self.left = src, dst, right, left
            self.units = [None] * 6

        def one(self, unit):
            to = self.right if unit in (0, 2, 4) else self.left
            self.units[unit] = send(self.src(unit), self.dst(unit), to)

        def start(self):
            for unit in (0, 1, 2, 3):
                self.one(unit)

        def relay(self, add):
            self.units[0].wait_recv()
            add(0)
            self.one(4)
            self.units[1].wait_recv()
            add(1)
            self.one(5)

        def finish(self):
            for unit in (2, 3, 4, 5):
                self.units[unit].wait_recv()

    load_x = local(x_hbm, xbuf)
    load_g = local(g_hbm, gbuf)
    weights = (wg_hbm, wu_hbm, wd_hbm)
    load_w = [local(w, wcat.at[j, :, pl.ds(0, HID)]) for j, w in enumerate(weights)]

    barrier = pltpu.get_barrier_semaphore()
    peers = [a_right, a_left, b_right, b_left, partner, sibling] + z_at[1:]
    for peer in peers:
        pl.semaphore_signal(barrier, inc=1, device_id=peer, device_id_type=MESH)

    row = lax.broadcasted_iota(jnp.int32, (16, 128), 0)
    col = lax.broadcasted_iota(jnp.int32, (16, 128), 1)
    pick = jnp.zeros((16, 128), F32)
    for s in range(SLOTS):
        pick = jnp.where((row == s) & (col == slot_ref[s]), 1.0, pick)
    router_rows = jnp.sum(pick[:SLOTS] * router_ref[...].astype(F32), axis=1, keepdims=True)
    router_tile = jnp.broadcast_to(router_rows, (SLOTS, EXTRA)).astype(BF)
    pick = pick.astype(BF)
    quarters = [pl.ds(pl.multiple_of(lax.rem(m + OFFSET[p], 4) * QUARTER, 128), QUARTER) for p in range(4)]

    def rows_of(buf, p):
        got = jnp.dot(pick, buf[:, quarters[p]], preferred_element_type=F32)
        return got[:SLOTS]

    load_x.wait()
    own_x = rows_of(xbuf, 0)
    for p in (1, 2, 3):
        stage_x[p, :, 0:QUARTER] = rows_of(xbuf, p).astype(BF)
        stage_x[p, :, QUARTER:WIDE] = router_tile
    load_g.wait()
    own_g = rows_of(gbuf, 0)
    for p in (1, 2, 3):
        stage_g[p] = rows_of(gbuf, p).astype(BF)
    stage_x[0, :, 0:QUARTER] = own_x.astype(BF)
    stage_x[0, :, QUARTER:WIDE] = router_tile
    stage_g[0] = own_g.astype(BF)

    pl.semaphore_wait(barrier, len(peers))

    first_x = [send(stage_x.at[p], land_x.at[MIRROR[p]], z_at[p]) for p in (3, 1, 2)]
    first_g = [send(stage_g.at[p], land_g.at[MIRROR[p]], z_at[p]) for p in (3, 1, 2)]
    sent_w = [send(w, wcat.at[j, :, pl.ds(HID, HID)], sibling) for j, w in enumerate(weights)]

    def make_shard(stage, land, out):
        parts = [stage[0].astype(F32)] + [land[p].astype(F32) for p in (1, 2, 3)]
        out[0:16] = jnp.concatenate(parts[0:2], axis=0).astype(BF)
        out[16:32] = jnp.concatenate(parts[2:4], axis=0).astype(BF)

    arrays = (xa, ga)
    gather_b = [Gather(lambda p, h, t=t: t.at[p, 0, h], b_right, b_left) for t in arrays]
    gather_a = [
        [Gather(lambda p, h, t=t, k=k: t.at[k, p, h], a_right, a_left) for t in arrays] for k in range(4)
    ]

    pair = []
    for i, (stage, land, first) in enumerate(((stage_x, land_x, first_x), (stage_g, land_g, first_g))):
        for copy in first:
            copy.wait_recv()
        make_shard(stage, land, arrays[i].at[0, 0, 0])
        pair.append(send(arrays[i].at[0, 0, 0], arrays[i].at[0, 0, 1], partner))
        gather_a[0][i].start(0)
        gather_b[i].start(0)
    for i in range(2):
        pair[i].wait_recv()
        gather_a[0][i].start(1)
        gather_b[i].start(1)

    reduce_z = [Reduce(lambda u, k=k: zs.at[k, u], lambda u, k=k: zr.at[k, u], z_right, z_left) for k in range(4)]
    gather_z = [Gather(lambda p, h, k=k: dl.at[k, p, h], z_right, z_left) for k in range(4)]
    reduce_a = [Reduce(lambda u, k=k: es.at[k, u], lambda u, k=k: er.at[k, u], a_right, a_left) for k in range(4)]
    reduce_b = Reduce(lambda u: fs.at[u], lambda u: fr.at[u], b_right, b_left)

    def encode(ref, j, v):
        exps = []
        for n in range(4):
            rows = v[8 * n : 8 * n + 8]
            top = jnp.max(jnp.abs(rows), axis=0, keepdims=True)
            exps.append(jnp.ceil(jnp.log2(jnp.maximum(top, 1e-30))))
        ups = [jnp.exp2(-e) * STEPS for e in exps]
        scaled = jnp.concatenate([v[8 * n : 8 * n + 8] * ups[n] for n in range(4)], axis=0)
        ref[pl.ds(32 * j, 32)] = jnp.floor(scaled + 0.5).astype(I32).astype(I16)
        return exps

    def put_exps(ref, exps):
        rows = jnp.concatenate(exps + [jnp.zeros((4, 256), F32)], axis=0)
        ref[pl.ds(96, 16)] = rows.astype(I32).astype(I16)

    def decode(ref):
        steps = jnp.exp2(ref[pl.ds(96, 16)].astype(I32).astype(F32)) * (1.0 / STEPS)
        v = ref[pl.ds(0, 96)].astype(I32).astype(F32)
        out = []
        for j in range(3):
            out.append(
                jnp.concatenate(
                    [v[8 * n : 8 * n + 8] * steps[n : n + 1] for n in range(4 * j, 4 * j + 4)], axis=0
                )
            )
        return out

    def forward(k):
        exps = [[], [], [], []]
        lhs_x = xa[k, :, :, :, 0:QUARTER].reshape(256, QUARTER)
        lhs_g = ga[k].reshape(256, QUARTER)
        for j, lhs in enumerate((lhs_x, lhs_x, lhs_g)):
            pre = jnp.dot(lhs, wcat[j], preferred_element_type=F32)
            piece = [
                [
                    jnp.concatenate([pre[(q * 4 + p) * 8 : (q * 4 + p) * 8 + 8] for q in range(4 * h, 4 * h + 4)], axis=0)
                    for h in range(2)
                ]
                for p in range(4)
            ]
            for u, v in enumerate((piece[OPP][0], piece[OPP][1], piece[RIGHT][1], piece[LEFT][0])):
                exps[u] += encode(zs.at[k, u], j, v)
            pre_own[k, 0, j] = piece[0][0]
            pre_own[k, 1, j] = piece[0][1]
            pre_right[k, j] = piece[RIGHT][0]
            pre_left[k, j] = piece[LEFT][1]
        for u in range(4):
            put_exps(zs.at[k, u], exps[u])
        reduce_z[k].start()

    def relay_z(k):
        def add(side):
            mine = pre_left if side else pre_right
            exps = []
            for j, v in enumerate(decode(zr.at[k, side])):
                exps += encode(zs.at[k, 4 + side], j, mine[k, j] + v)
            put_exps(zs.at[k, 4 + side], exps)

        reduce_z[k].relay(add)

    def elementwise(k):
        reduce_z[k].finish()
        for h in range(2):
            near, far = (2, 5) if h else (3, 4)
            first, second = decode(zr.at[k, near]), decode(zr.at[k, far])
            gate_pre, up_pre, act_grad = [pre_own[k, h, j] + first[j] + second[j] for j in range(3)]
            router = xa[k, 2 * h : 2 * h + 2, :, 0:16, QUARTER:WIDE].astype(F32)[:, :, 0:8].reshape(32, EXTRA)
            router = jnp.concatenate([router, router], axis=1)
            sigmoid_g = jax.nn.sigmoid(gate_pre)
            active = sigmoid_g * gate_pre * up_pre
            dl[k, 0, h, 2] = (router * active).astype(BF)
            act_delta = router * act_grad
            dl[k, 0, h, 0] = (act_delta * up_pre * sigmoid_g * (1.0 + gate_pre * (1.0 - sigmoid_g))).astype(BF)
            dl[k, 0, h, 1] = (act_delta * sigmoid_g * gate_pre).astype(BF)
            product = active * act_grad
            router_part[k, pl.ds(32 * h, 32)] = product[:, 0:128] + product[:, 128:256]
            gather_z[k].start(h)

    def extra_of(v):
        high = v.astype(BF)
        low = (v - high.astype(F32)).astype(BF)
        return jnp.concatenate([high.astype(F32), low.astype(F32), jnp.zeros((16, EXTRA), F32)], axis=0)

    def backward(k):
        for j in range(3):
            d = dl[k, :, :, j].astype(F32)
            parts = []
            for q in range(8):
                for p in range(4):
                    parts.append(d[p, q // 4, (q % 4) * 8 : (q % 4) * 8 + 8])
            dmat[j, pl.ds(256 * k, 256)] = jnp.concatenate(parts, axis=0).astype(BF)

        def block(n, carry):
            cols = pl.ds(pl.multiple_of(n * 256, 256), 256)
            nt = (((1,), (1,)), ((), ()))
            rows = pl.ds(256 * k, 256)
            dx = lax.dot_general(dmat[0, rows], wcat[0, cols, :], nt, preferred_element_type=F32)
            dx = dx + lax.dot_general(dmat[1, rows], wcat[1, cols, :], nt, preferred_element_type=F32)
            unit = [dx[32 * q : 32 * q + 32] for q in range(8)]
            e_own[k, 0, :, cols] = unit[0]
            e_own[k, 1, :, cols] = unit[1]
            e_right[k, :, cols] = unit[2]
            es[k, 2, :, cols] = unit[3].astype(BF)
            es[k, 3, :, cols] = unit[4].astype(BF)
            e_left[k, :, cols] = unit[5]
            es[k, 0, :, cols] = unit[6].astype(BF)
            es[k, 1, :, cols] = unit[7].astype(BF)
            return carry

        lax.fori_loop(0, QUARTER // 256, block, 0)
        tail = slice(QUARTER, WIDE)
        ex = [extra_of(router_part[k, pl.ds(8 * q, 8)]) for q in range(8)]
        e_own[k, 0, :, tail] = ex[0]
        e_own[k, 1, :, tail] = ex[1]
        e_right[k, :, tail] = ex[2]
        es[k, 2, :, tail] = ex[3].astype(BF)
        es[k, 3, :, tail] = ex[4].astype(BF)
        e_left[k, :, tail] = ex[5]
        es[k, 0, :, tail] = ex[6].astype(BF)
        es[k, 1, :, tail] = ex[7].astype(BF)
        reduce_a[k].start()

    def put(ref, total):
        ref[:, 0:QUARTER] = total[:, 0:QUARTER].astype(BF)
        v = total[0:8, QUARTER:WIDE] + total[8:16, QUARTER:WIDE]
        ref[:, QUARTER:WIDE] = extra_of(v).astype(BF)

    def relay_a(k):
        def add(side):
            mine = e_left if side else e_right
            put(es.at[k, 4 + side], mine[k] + er[k, side].astype(F32))

        reduce_a[k].relay(add)

    def finish_a(k):
        reduce_a[k].finish()
        total = [
            e_own[k, h] + er[k, (3, 2)[h]].astype(F32) + er[k, (4, 5)[h]].astype(F32) for h in range(2)
        ]
        if k == 0:
            f_own[0] = total[0]
            f_own[1] = total[1]
        elif k == RIGHT:
            f_right[...] = total[0]
            put(fs.at[2], total[1])
            reduce_b.one(2)
        elif k == LEFT:
            put(fs.at[3], total[0])
            f_left[...] = total[1]
            reduce_b.one(3)
        else:
            put(fs.at[0], total[0])
            reduce_b.one(0)
            put(fs.at[1], total[1])
            reduce_b.one(1)

    def start_a(k):
        for i in range(2):
            if k == RIGHT:
                gather_b[i].finish_right()
            elif k == LEFT:
                gather_b[i].finish_left()
            else:
                gather_b[i].finish_opposite()
            gather_a[k][i].start(0)
            gather_a[k][i].start(1)

    def relay_gather(k):
        for i in range(2):
            gather_a[k][i].relay()

    def finish_gather(k):
        for i in range(2):
            gather_a[k][i].finish()

    part = []

    def weight_block(n, carry):
        cols = pl.ds(pl.multiple_of(n * 256, 256), 256)
        tn = (((0,), (0,)), ((), ()))
        lhs_x = xa[:, :, :, :, cols].reshape(1024, 256)
        lhs_g = ga[:, :, :, :, cols].reshape(1024, 256)
        for j, lhs in enumerate((lhs_x, lhs_x, lhs_g)):
            dw = lax.dot_general(lhs, dmat[j], tn, preferred_element_type=F32)
            own_part[j, cols, :] = dw[:, 0:HID]
            part_send[j, cols, :] = dw[:, HID:]
        return carry

    def weight_grads():
        lax.fori_loop(0, QUARTER // 256, weight_block, 0)
        for j in range(3):
            part.append(send(part_send.at[j], peer_part.at[j], sibling))

    for i in range(2):
        gather_a[0][i].relay()
        gather_b[i].relay()
    start_a(RIGHT)
    finish_gather(0)
    for copy in load_w:
        copy.wait()
    for copy in sent_w:
        copy.wait_recv()
    forward(0)
    relay_gather(1)
    start_a(LEFT)
    relay_z(0)
    finish_gather(1)
    forward(1)
    elementwise(0)
    relay_gather(2)
    start_a(OPP)
    relay_z(1)
    gather_z[0].relay()
    elementwise(1)
    finish_gather(2)
    forward(2)
    gather_z[0].finish()
    backward(0)
    relay_gather(3)
    relay_z(2)
    gather_z[1].relay()
    relay_a(0)
    elementwise(2)
    finish_gather(3)
    forward(3)
    gather_z[1].finish()
    backward(1)
    relay_z(3)
    gather_z[2].relay()
    relay_a(1)
    finish_a(0)
    elementwise(3)
    gather_z[2].finish()
    backward(2)
    gather_z[3].relay()
    relay_a(2)
    finish_a(1)
    gather_z[3].finish()
    backward(3)
    finish_a(2)
    relay_a(3)
    weight_grads()
    finish_a(3)

    def add_b(side):
        mine = f_left if side else f_right
        put(fs.at[4 + side], mine[...] + fr[side].astype(F32))

    reduce_b.relay(add_b)
    reduce_b.finish()
    for h in (1, 0):
        total = f_own[h] + fr[(3, 2)[h]].astype(F32) + fr[(4, 5)[h]].astype(F32)
        if h:
            put(zl_send, total)
            swap = send(zl_send, zl_recv, partner)
        else:
            f_own[0] = total
    swap.wait_recv()
    total = f_own[0] + zl_recv[...].astype(F32)
    router_sum = total[0:8, QUARTER:WIDE] + total[8:16, QUARTER:WIDE]
    for p in range(4):
        last_send[p] = total[8 * p : 8 * p + 8, 0:QUARTER].astype(BF)
    last = [send(last_send.at[p], last_recv.at[MIRROR[p]], z_at[p]) for p in (3, 1, 2)]

    hit = lax.broadcasted_iota(jnp.int32, (SLOTS, 128), 0) == token_ref[...]
    router_rows = jnp.sum(router_sum, axis=1, keepdims=True)
    router_out[...] = jnp.sum(jnp.where(hit, router_rows, 0.0), axis=0, keepdims=True)
    hot = jnp.concatenate([jnp.where(hit, 1.0, 0.0), jnp.zeros((SLOTS, 128), F32)], axis=0).astype(BF)
    stores = []

    def place(p, rows):
        rows = jnp.concatenate([rows.astype(F32), jnp.zeros((SLOTS, QUARTER), F32)], axis=0).astype(BF)
        spread = lax.dot_general(hot, rows, (((0,), (0,)), ((), ())), preferred_element_type=F32)
        xbuf[:, quarters[p]] = spread.astype(BF)

    place(0, last_send[0])
    for j, out in enumerate((gate_out, up_out, down_out)):
        part[j].wait_recv()
        own_part[j] = own_part[j] + peer_part[j]
        stores.append(local(own_part.at[j], out))
    for p, copy in zip((2, 1, 3), (last[1], last[2], last[0])):
        copy.wait_recv()
        place(p, last_recv[p])
    stores.append(local(xbuf, input_out))
    for copy in stores:
        copy.wait()
    for copy in sent:
        copy.wait_send()


def local_step(
    layer_input,
    out_grad,
    router_weight,
    token_slot,
    slot_token,
    gate_weight,
    up_weight,
    down_weight,
):
    any_ = pl.BlockSpec(memory_space=pl.ANY)
    vmem = pl.BlockSpec(memory_space=pltpu.VMEM)
    grad = jax.ShapeDtypeStruct((QUARTER, HID), F32)
    input_grad, router, gate_grad, up_grad, down_grad = pl.pallas_call(
        kernel,
        out_shape=(
            jax.ShapeDtypeStruct((128, 4 * QUARTER), BF),
            jax.ShapeDtypeStruct((1, 128), F32),
            grad,
            grad,
            grad,
        ),
        in_specs=[pl.BlockSpec(memory_space=pltpu.SMEM), vmem, vmem, any_, any_, any_, any_, any_],
        out_specs=(any_, vmem, any_, any_, any_),
        scratch_shapes=[
            pltpu.VMEM((128, 4 * QUARTER), BF),
            pltpu.VMEM((128, 4 * QUARTER), BF),
            pltpu.VMEM((3, QUARTER, 2 * HID), BF),
            pltpu.VMEM((4, SLOTS, WIDE), BF),
            pltpu.VMEM((4, SLOTS, QUARTER), BF),
            pltpu.VMEM((4, SLOTS, WIDE), BF),
            pltpu.VMEM((4, SLOTS, QUARTER), BF),
            pltpu.VMEM((4, 4, 2, SHARD, WIDE), BF),
            pltpu.VMEM((4, 4, 2, SHARD, QUARTER), BF),
            pltpu.VMEM((4, 2, 3, 32, 256), F32),
            pltpu.VMEM((4, 3, 32, 256), F32),
            pltpu.VMEM((4, 3, 32, 256), F32),
            pltpu.VMEM((4, 6, CODED, 256), I16),
            pltpu.VMEM((4, 6, CODED, 256), I16),
            pltpu.VMEM((4, 4, 2, 3, 32, 256), BF),
            pltpu.VMEM((4, 64, EXTRA), F32),
            pltpu.VMEM((3, 1024, 256), BF),
            pltpu.VMEM((4, 2, SHARD, WIDE), F32),
            pltpu.VMEM((4, SHARD, WIDE), F32),
            pltpu.VMEM((4, SHARD, WIDE), F32),
            pltpu.VMEM((4, 6, SHARD, WIDE), BF),
            pltpu.VMEM((4, 6, SHARD, WIDE), BF),
            pltpu.VMEM((2, SHARD, WIDE), F32),
            pltpu.VMEM((SHARD, WIDE), F32),
            pltpu.VMEM((SHARD, WIDE), F32),
            pltpu.VMEM((6, SHARD, WIDE), BF),
            pltpu.VMEM((6, SHARD, WIDE), BF),
            pltpu.VMEM((SHARD, WIDE), BF),
            pltpu.VMEM((SHARD, WIDE), BF),
            pltpu.VMEM((4, SLOTS, QUARTER), BF),
            pltpu.VMEM((4, SLOTS, QUARTER), BF),
            pltpu.VMEM((3, QUARTER, HID), F32),
            pltpu.VMEM((3, QUARTER, HID), F32),
            pltpu.VMEM((3, QUARTER, HID), F32),
            pltpu.SemaphoreType.DMA((UNITS,)),
            pltpu.SemaphoreType.DMA((UNITS,)),
            pltpu.SemaphoreType.DMA((16,)),
        ],
        compiler_params=pltpu.CompilerParams(
            collective_id=0, has_side_effects=True, vmem_limit_bytes=60 * 1024 * 1024
        ),
    )(
        slot_token,
        router_weight[None, :],
        token_slot[None, :],
        layer_input,
        out_grad,
        gate_weight,
        up_weight,
        down_weight,
    )
    return (input_grad, router[0], gate_grad, up_grad, down_grad)


def solution(mesh):
    both = ("dp", "ckpt")
    return jax.shard_map(
        local_step,
        mesh=mesh,
        in_specs=(
            P(both, None),
            P(both, None),
            P(both),
            P(both),
            P(both),
            P("ckpt", "dp"),
            P("ckpt", "dp"),
            P("ckpt", "dp"),
        ),
        out_specs=(P(both, None), P(both), P("ckpt", "dp"), P("ckpt", "dp"), P("ckpt", "dp")),
        check_vma=False,
    )
```
